32 devices in a mesh: img: 8 (over z, y), txt: 4 (over x, core).
Axes of the slice: x: 2, y: 2, z: 4, core: 2. Of those that a mesh axis runs over, the one named last changes fastest.
Arguments:
- images: float32 [1024, 1024], P(('img', 'txt')), may hold values from -1 to 1
- texts: float32 [1024, 1024], P(('txt', 'img')), may hold values from -1 to 1
- labels: int32 [1024], P('img'), may hold values from 0 to 1023, each once
Outputs:
- row_loss: float32 [1024], P('img')
- image_grad: float32 [1024, 1024], P(('img', 'txt'))
- text_grad: float32 [1024, 1024], P(('txt', 'img'))
The draws below stay inside these ranges and needn't reach their ends.
Inputs may be any that keep to these rules, and one draw needn't show every extreme that they name: `labels`: each text index appears exactly once.
All inputs are finite; a program needn't handle non-finite values.
Results may differ from the reference program's by a relative error of at most 0.017.
Values may be sent and summed in bfloat16 or wider, within the bound.
A program may use at most 64 MiB of HBM per device.

```python
import jax
import jax.numpy as jnp
from jax import lax

WIDTH = 1024
IMG_BLK = 128
TXT_BLK = 256
BATCH = 1024
N_IMG = 8
N_TXT = 4


def draw_both(key):
    key_text = jax.random.fold_in(key, 11)
    key_image = jax.random.fold_in(key, 12)
    spread = WIDTH ** (-0.5)
    texts = jax.random.truncated_normal(key_text, -5.0, 5.0, (BATCH, WIDTH), jnp.float32) * spread
    images = jax.random.truncated_normal(key_image, -5.0, 5.0, (BATCH, WIDTH), jnp.float32) * spread
    return (images, texts)


def draw_images(key, part):
    return draw_both(key)[0]


def draw_texts(key, part):
    return draw_both(key)[1]


def setup_inputs(seed: int = 0) -> dict:
    seeds = jax.random.split(jax.random.key(seed), 4)
    return {
        "images": draw_images(jax.random.fold_in(seeds[3], 71), 0),
        "texts": draw_texts(jax.random.fold_in(seeds[3], 71), 0),
        "labels": jax.random.permutation(seeds[2], BATCH).astype(jnp.int32),
    }


logit_scale = 100.0


def reference(images, texts, labels):
    image_low = images.astype(jnp.bfloat16)
    text_low = texts.astype(jnp.bfloat16)
    image_blocks = image_low.reshape(N_IMG, IMG_BLK, WIDTH)
    label_blocks = labels.reshape(N_IMG, IMG_BLK)
    columns = jnp.arange(BATCH, dtype=jnp.int32)
    text_split = text_low.reshape(N_TXT, TXT_BLK, WIDTH).astype(jnp.float32)

    def block_step(carry, inputs):
        block, block_labels = inputs
        logits = logit_scale * jnp.dot(block, text_low.T, preferred_element_type=jnp.float32)
        highest = jnp.max(logits, axis=1)
        exp_total = jnp.sum(jnp.exp(logits - highest[:, None]), axis=1)
        log_total = highest + jnp.log(exp_total)
        hits = columns[None, :] == block_labels[:, None]
        positive = jnp.sum(jnp.where(hits, logits, 0.0), axis=1)
        losses = log_total - positive
        grad_tile = (logit_scale * (jnp.exp(logits - log_total[:, None]) - hits.astype(jnp.float32))).astype(jnp.bfloat16)
        pieces = jnp.einsum("rnc,ncd->nrd", grad_tile.reshape(IMG_BLK, N_TXT, TXT_BLK).astype(jnp.float32), text_split)
        image_part = jnp.sum(pieces.astype(jnp.bfloat16).astype(jnp.float32), axis=0)
        text_part = jnp.dot(grad_tile.T, block, preferred_element_type=jnp.float32)
        return carry + text_part.astype(jnp.bfloat16).astype(jnp.float32), (losses, image_part)

    start = jnp.zeros((BATCH, WIDTH), jnp.float32)
    text_grad, (losses, image_parts) = lax.scan(block_step, start, (image_blocks, label_blocks))
    return losses.reshape(BATCH), image_parts.reshape(BATCH, WIDTH), text_grad
```

```python
import functools

import jax
import jax.numpy as jnp
from jax import lax
from jax.experimental import pallas as pl
from jax.experimental.pallas import tpu as pltpu
from jax.sharding import PartitionSpec as P

logit_scale = 100.0
MESH = pl.DeviceIdType.MESH


def kernel(
    n_img, n_txt,
    labels_ref, images_hbm, texts_hbm,
    loss_ref, image_grad_ref, text_grad_ref,
    images_in, texts_in, img_panel, txt_panel, stats, text_terms, from_pair, paired,
    from_line, image_terms, from_txt,
    load_sems, send_sems, txt_sems, img_sems, stat_sems, pair_sems, line_sems, term_sems,
):
    length = n_img // 2
    rows, width = images_in.shape
    img, txt = lax.axis_index("img"), lax.axis_index("txt")
    z, y = img // 2, img % 2
    c = txt % 2
    across = (z * 2 + (1 - y), txt)
    partner = (img, txt - c + (1 - c))
    up, down = ((z + 1) * 2 + y, txt), ((z - 1) * 2 + y, txt)
    has_up, has_down = z < length - 1, z > 0

    loads = [
        pltpu.make_async_copy(images_hbm, images_in, load_sems.at[0]),
        pltpu.make_async_copy(texts_hbm, texts_in, load_sems.at[1]),
    ]
    for load in loads:
        load.start()

    barrier = pltpu.get_barrier_semaphore()
    others = [(img, lax.rem(txt + k, n_txt)) for k in range(1, n_txt)]
    for device in [across] + others:
        pl.semaphore_signal(barrier, inc=1, device_id=device, device_id_type=MESH)

    @pl.when(has_up)
    def _():
        pl.semaphore_signal(barrier, inc=1, device_id=up, device_id_type=MESH)

    @pl.when(has_down)
    def _():
        pl.semaphore_signal(barrier, inc=1, device_id=down, device_id_type=MESH)

    loads[1].wait()
    txt_panel[0, z] = texts_in[...].astype(jnp.bfloat16)
    loads[0].wait()
    img_panel[txt] = images_in[...].astype(jnp.bfloat16)
    pl.semaphore_wait(barrier, n_txt + jnp.where(has_up, 1, 0) + jnp.where(has_down, 1, 0))

    sent = []

    def guarded(condition, act):
        if condition is None:
            act()
        else:
            pl.when(condition)(act)

    def push(src, dst, arrival, device, condition=None):
        number = len(sent)

        def copy():
            return pltpu.make_async_remote_copy(
                src_ref=src(), dst_ref=dst(), send_sem=send_sems.at[number], recv_sem=arrival(),
                device_id=device, device_id_type=MESH,
            )

        sent.append((condition, copy))
        guarded(condition, lambda: copy().start())

    def arrived(ref, arrival, condition=None):
        def act():
            pltpu.make_async_remote_copy(
                src_ref=ref(), dst_ref=ref(), send_sem=send_sems.at[0], recv_sem=arrival(),
                device_id=across, device_id_type=MESH,
            ).wait_recv()

        guarded(condition, act)

    def push_text(source, side, device, condition=None):
        push(
            lambda: txt_panel.at[0, source], lambda: txt_panel.at[side, source],
            lambda: txt_sems.at[side, source], device, condition,
        )

    def push_image(source, device):
        push(
            lambda: img_panel.at[source], lambda: img_panel.at[source],
            lambda: img_sems.at[source], device,
        )

    def image_arrived(source):
        arrived(lambda: img_panel.at[source], lambda: img_sems.at[source])

    push_text(z, 0, up, has_up)
    push_text(z, 0, down, has_down)
    push_text(z, 1, across)
    same_side = [lax.rem(txt + 2 * k, n_txt) for k in range(1, n_txt // 2)]
    for other in same_side:
        push_image(txt, (img, other))
    push_image(txt, partner)

    for step in range(1, length):
        for source, onward, more in ((z - step, up, has_up), (z + step, down, has_down)):
            there = jnp.logical_and(source >= 0, source < length)
            arrived(
                lambda source=source: txt_panel.at[0, source],
                lambda source=source: txt_sems.at[0, source], there,
            )
            push_text(source, 0, onward, jnp.logical_and(there, more))
            push_text(source, 1, across, there)
        if step == 1:
            for other in same_side:
                image_arrived(other)
                push_image(other, partner)
    image_arrived(partner[1])
    for other in same_side:
        image_arrived(other - c + (1 - c))
    for source in range(length):
        arrived(lambda: txt_panel.at[1, source], lambda: txt_sems.at[1, source])

    text_rows, image_rows = n_img * rows, n_txt * rows
    image_low = img_panel[...].reshape(image_rows, width)
    text_low = txt_panel[...].reshape(text_rows, width)
    logits = logit_scale * lax.dot_general(
        text_low, image_low, (((1,), (1,)), ((), ())), preferred_element_type=jnp.float32
    )
    place = lax.broadcasted_iota(jnp.int32, (text_rows, 1), 0)
    side = place // (length * rows)
    block = (place // rows) % length
    column = txt * text_rows + (block * 2 + jnp.where(side == 0, y, 1 - y)) * rows + place % rows
    hits = column == labels_ref[...]
    highest = jnp.max(logits, axis=0, keepdims=True)
    exp_total = jnp.sum(jnp.exp(logits - highest), axis=0, keepdims=True)
    positive = jnp.sum(jnp.where(hits, logits, 0.0), axis=0, keepdims=True)
    line = lax.broadcasted_iota(jnp.int32, stats.shape[1:], 0)
    stats[txt] = jnp.where(
        line == 0, highest, jnp.where(line == 1, exp_total, jnp.where(line == 2, positive, 0.0))
    )
    for device in others:
        push(
            lambda: stats.at[txt], lambda: stats.at[txt], lambda: stat_sems.at[txt], device
        )
    for device in others:
        arrived(lambda: stats.at[device[1]], lambda: stat_sems.at[device[1]])
    every = stats[...]
    tops = every[:, 0:1, :]
    top = jnp.max(tops, axis=0)
    total = jnp.sum(every[:, 1:2, :] * jnp.exp(tops - top[None]), axis=0)
    log_total = top + jnp.log(total)
    loss_ref[...] = log_total - jnp.sum(every[:, 2:3, :], axis=0)
    grad_tile = (
        logit_scale * (jnp.exp(logits - log_total) - hits.astype(jnp.float32))
    ).astype(jnp.bfloat16)

    half = length * rows

    def side_terms(side):
        text_terms[side] = (
            jnp.dot(
                grad_tile[side * half : (side + 1) * half], image_low,
                preferred_element_type=jnp.float32,
            )
            .astype(jnp.bfloat16)
            .reshape(length, rows, width)
        )

    far_first = []
    for step in range(length - 1, 0, -1):
        for target in (z + step, z - step):
            far_first.append((target, jnp.logical_and(target >= 0, target < length)))
    side_terms(1)
    for target, there in far_first + [(z, None)]:
        push(
            lambda target=target: text_terms.at[1, target],
            lambda target=target: from_pair.at[target],
            lambda target=target: pair_sems.at[target], across, there,
        )
    image_terms[...] = (
        lax.dot_general(
            grad_tile, text_low, (((0,), (0,)), ((), ())), preferred_element_type=jnp.float32
        )
        .astype(jnp.bfloat16)
        .reshape(n_txt, rows, width)
    )
    for device in others:
        push(
            lambda device=device: image_terms.at[device[1]], lambda: from_txt.at[txt],
            lambda: term_sems.at[txt], device,
        )
    side_terms(0)

    def pair_sum(target):
        return text_terms[0, target].astype(jnp.float32) + from_pair[target].astype(jnp.float32)

    for target, there in far_first:
        arrived(
            lambda target=target: from_pair.at[target],
            lambda target=target: pair_sems.at[target], there,
        )

        def add(target=target):
            paired[target] = pair_sum(target).astype(jnp.bfloat16)

        guarded(there, add)
        push(
            lambda target=target: paired.at[target], lambda: from_line.at[z],
            lambda: line_sems.at[z], (target * 2 + y, txt), there,
        )

    for device in others:
        arrived(lambda: from_txt.at[device[1]], lambda: term_sems.at[device[1]])
    image_sum = image_terms[txt].astype(jnp.float32)
    for device in others:
        image_sum += from_txt[device[1]].astype(jnp.float32)
    image_grad_ref[...] = image_sum

    arrived(lambda: from_pair.at[z], lambda: pair_sems.at[z])
    text_grad_ref[...] = pair_sum(z)
    for source, there in far_first[::-1]:
        def add(source=source):
            arrived(lambda: from_line.at[source], lambda: line_sems.at[source])
            text_grad_ref[...] += from_line[source].astype(jnp.float32)

        guarded(there, add)

    for condition, copy in sent:
        guarded(condition, lambda: copy().wait_send())


def local(n_img, n_txt, images, texts, labels):
    rows, width = images.shape
    length = n_img // 2
    image_rows = labels.shape[0]
    vmem = pl.BlockSpec(memory_space=pltpu.VMEM)
    hbm = pl.BlockSpec(memory_space=pl.ANY)
    low = jnp.bfloat16
    dma = pltpu.SemaphoreType.DMA
    sends = 3 + n_txt + 4 * length + 2 * (n_txt - 1) + 4 * length + n_txt
    loss, image_grad, text_grad = pl.pallas_call(
        functools.partial(kernel, n_img, n_txt),
        out_shape=(
            jax.ShapeDtypeStruct((1, image_rows), jnp.float32),
            jax.ShapeDtypeStruct((rows, width), jnp.float32),
            jax.ShapeDtypeStruct((rows, width), jnp.float32),
        ),
        in_specs=[vmem, hbm, hbm],
        out_specs=(vmem, vmem, vmem),
        scratch_shapes=[
            pltpu.VMEM((rows, width), jnp.float32),
            pltpu.VMEM((rows, width), jnp.float32),
            pltpu.VMEM((n_txt, rows, width), low),
            pltpu.VMEM((2, length, rows, width), low),
            pltpu.VMEM((n_txt, 8, image_rows), jnp.float32),
            pltpu.VMEM((2, length, rows, width), low),
            pltpu.VMEM((length, rows, width), low),
            pltpu.VMEM((length, rows, width), low),
            pltpu.VMEM((length, rows, width), low),
            pltpu.VMEM((n_txt, rows, width), low),
            pltpu.VMEM((n_txt, rows, width), low),
            dma((2,)),
            dma((sends,)),
            dma((2, length)),
            dma((n_txt,)),
            dma((n_txt,)),
            dma((length,)),
            dma((length,)),
            dma((n_txt,)),
        ],
        compiler_params=pltpu.CompilerParams(
            collective_id=0, has_side_effects=True, vmem_limit_bytes=48 * 1024 * 1024
        ),
    )(labels.reshape(1, image_rows), images, texts)
    return loss.reshape(image_rows), image_grad, text_grad


def solution(mesh):
    in_specs = (P(("img", "txt"), None), P(("txt", "img"), None), P("img"))
    out_specs = (P("img"), P(("img", "txt"), None), P(("txt", "img"), None))
    body = functools.partial(local, mesh.shape["img"], mesh.shape["txt"])
    return jax.shard_map(body, mesh=mesh, in_specs=in_specs, out_specs=out_specs, check_vma=False)
```

```python
import functools

import jax
import jax.numpy as jnp
from jax import lax
from jax.experimental import pallas as pl
from jax.experimental.pallas import tpu as pltpu
from jax.sharding import PartitionSpec as P

logit_scale = 100.0
MESH = pl.DeviceIdType.MESH
parts = 2


def kernel(
    n_img, n_txt,
    labels_hbm, images_hbm, texts_hbm,
    loss_ref, image_grad_ref, text_grad_ref,
    labels_ref, images_in, texts_in, img_panel, txt_panel, stats, text_terms, from_pair, paired,
    from_line, image_terms, from_txt,
    load_sems, send_sems, txt_sems, img_sems, stat_sems, pair_sems, line_sems, term_sems,
):
    length = n_img // 2
    rows, width = images_in.shape
    img, txt = lax.axis_index("img"), lax.axis_index("txt")
    z, y = img // 2, img % 2
    c = txt % 2
    across = (z * 2 + (1 - y), txt)
    partner = (img, txt - c + (1 - c))
    piece = rows // parts
    pieces = [pl.ds(part * piece, piece) for part in range(parts)]

    loads = [
        pltpu.make_async_copy(images_hbm, images_in, load_sems.at[0]),
        pltpu.make_async_copy(texts_hbm, texts_in, load_sems.at[1]),
        pltpu.make_async_copy(labels_hbm, labels_ref, load_sems.at[2]),
    ]
    for load in loads:
        load.start()

    barrier = pltpu.get_barrier_semaphore()
    others = [(img, lax.rem(txt + k, n_txt)) for k in range(1, n_txt)]
    for device in [across] + others:
        pl.semaphore_signal(barrier, inc=1, device_id=device, device_id_type=MESH)

    greeted = n_txt
    for place in (z + 1, z - 1, z + 2, z - 2):
        inside = jnp.logical_and(place >= 0, place < length)
        greeted += jnp.where(inside, 1, 0)

        @pl.when(inside)
        def _():
            pl.semaphore_signal(
                barrier, inc=1, device_id=(place * 2 + y, txt), device_id_type=MESH
            )

    loads[1].wait()
    txt_panel[0, z] = texts_in[...].astype(jnp.bfloat16)
    loads[0].wait()
    img_panel[txt] = images_in[...].astype(jnp.bfloat16)
    loads[2].wait()
    pl.semaphore_wait(barrier, greeted)

    sent = []

    def guarded(condition, act):
        if condition is None:
            act()
        else:
            pl.when(condition)(act)

    def push(src, dst, arrival, device, condition=None):
        number = len(sent)

        def copy():
            return pltpu.make_async_remote_copy(
                src_ref=src(), dst_ref=dst(), send_sem=send_sems.at[number], recv_sem=arrival(),
                device_id=device, device_id_type=MESH,
            )

        sent.append((condition, copy))
        guarded(condition, lambda: copy().start())

    def arrived(ref, arrival, condition=None):
        def act():
            pltpu.make_async_remote_copy(
                src_ref=ref(), dst_ref=ref(), send_sem=send_sems.at[0], recv_sem=arrival(),
                device_id=across, device_id_type=MESH,
            ).wait_recv()

        guarded(condition, act)

    def push_text(source, part, side, device, condition=None):
        push(
            lambda: txt_panel.at[0, source, pieces[part]],
            lambda: txt_panel.at[side, source, pieces[part]],
            lambda: txt_sems.at[side, source, part], device, condition,
        )

    def text_arrived(source, part, side, condition=None):
        arrived(
            lambda: txt_panel.at[side, source, pieces[part]],
            lambda: txt_sems.at[side, source, part], condition,
        )

    def pass_on(source, part, way, there=None):
        for reach in (1, 2):
            target = z + way * reach
            inside = jnp.logical_and(target >= 0, target < length)
            if there is not None:
                inside = jnp.logical_and(inside, there)
            push_text(source, part, 0, (target * 2 + y, txt), inside)

    def push_image(source, device):
        push(
            lambda: img_panel.at[source], lambda: img_panel.at[source],
            lambda: img_sems.at[source], device,
        )

    def image_arrived(source):
        arrived(lambda: img_panel.at[source], lambda: img_sems.at[source])

    for part in range(parts):
        push_text(z, part, 1, across)
        for way in (1, -1):
            pass_on(z, part, way)
    same_side = [lax.rem(txt + 2 * k, n_txt) for k in range(1, n_txt // 2)]
    for other in same_side:
        push_image(txt, (img, other))
    push_image(txt, partner)

    for step in range(1, length):
        for part in range(parts):
            for way in (1, -1):
                source = z - way * step
                there = jnp.logical_and(source >= 0, source < length)
                text_arrived(source, part, 0, there)
                if step % 2 == 0:
                    pass_on(source, part, way, there)
                push_text(source, part, 1, across, there)
        if step == 1:
            for other in same_side:
                image_arrived(other)
                push_image(other, partner)
    image_arrived(partner[1])
    for other in same_side:
        image_arrived(other - c + (1 - c))
    for source in range(length):
        for part in range(parts):
            text_arrived(source, part, 1)

    text_rows, image_rows = n_img * rows, n_txt * rows
    image_low = img_panel[...].reshape(image_rows, width)
    text_low = txt_panel[...].reshape(text_rows, width)
    logits = logit_scale * lax.dot_general(
        text_low, image_low, (((1,), (1,)), ((), ())), preferred_element_type=jnp.float32
    )
    place = lax.broadcasted_iota(jnp.int32, (text_rows, 1), 0)
    side = place // (length * rows)
    block = (place // rows) % length
    column = txt * text_rows + (block * 2 + jnp.where(side == 0, y, 1 - y)) * rows + place % rows
    hits = column == labels_ref[...]
    highest = jnp.max(logits, axis=0, keepdims=True)
    exp_total = jnp.sum(jnp.exp(logits - highest), axis=0, keepdims=True)
    positive = jnp.sum(jnp.where(hits, logits, 0.0), axis=0, keepdims=True)
    line = lax.broadcasted_iota(jnp.int32, stats.shape[1:], 0)
    stats[txt] = jnp.where(
        line == 0, highest, jnp.where(line == 1, exp_total, jnp.where(line == 2, positive, 0.0))
    )
    for device in others:
        push(
            lambda: stats.at[txt], lambda: stats.at[txt], lambda: stat_sems.at[txt], device
        )
    for device in others:
        arrived(lambda: stats.at[device[1]], lambda: stat_sems.at[device[1]])
    every = stats[...]
    tops = every[:, 0:1, :]
    top = jnp.max(tops, axis=0)
    total = jnp.sum(every[:, 1:2, :] * jnp.exp(tops - top[None]), axis=0)
    log_total = top + jnp.log(total)
    loss_ref[...] = log_total - jnp.sum(every[:, 2:3, :], axis=0)
    grad_tile = (
        logit_scale * (jnp.exp(logits - log_total) - hits.astype(jnp.float32))
    ).astype(jnp.bfloat16)

    half = length * rows

    def side_terms(side):
        text_terms[side] = (
            jnp.dot(
                grad_tile[side * half : (side + 1) * half], image_low,
                preferred_element_type=jnp.float32,
            )
            .astype(jnp.bfloat16)
            .reshape(length, rows, width)
        )

    far_first = []
    for step in range(length - 1, 0, -1):
        for target in (z + step, z - step):
            far_first.append((target, jnp.logical_and(target >= 0, target < length)))
    side_terms(1)
    def push_pair(target, part, there):
        push(
            lambda: text_terms.at[1, target, pieces[part]],
            lambda: from_pair.at[target, pieces[part]],
            lambda: pair_sems.at[target, part], across, there,
        )

    for target, there in far_first + [(z, None)]:
        for part in range(parts):
            push_pair(target, part, there)
    image_terms[...] = (
        lax.dot_general(
            grad_tile, text_low, (((0,), (0,)), ((), ())), preferred_element_type=jnp.float32
        )
        .astype(jnp.bfloat16)
        .reshape(n_txt, rows, width)
    )
    for device in others:
        push(
            lambda device=device: image_terms.at[device[1]], lambda: from_txt.at[txt],
            lambda: term_sems.at[txt], device,
        )
    side_terms(0)

    def pair_sum(target, part):
        return text_terms[0, target, pieces[part]].astype(jnp.float32) + from_pair[
            target, pieces[part]
        ].astype(jnp.float32)

    def pair_arrived(target, part, there=None):
        arrived(
            lambda: from_pair.at[target, pieces[part]],
            lambda: pair_sems.at[target, part], there,
        )

    def push_line(target, part, there):
        def add():
            paired[target, pieces[part]] = pair_sum(target, part).astype(jnp.bfloat16)

        pair_arrived(target, part, there)
        guarded(there, add)
        push(
            lambda: paired.at[target, pieces[part]], lambda: from_line.at[z, pieces[part]],
            lambda: line_sems.at[z, part], (target * 2 + y, txt), there,
        )

    for target, there in far_first:
        for part in range(parts):
            push_line(target, part, there)

    for device in others:
        arrived(lambda: from_txt.at[device[1]], lambda: term_sems.at[device[1]])
    image_sum = image_terms[txt].astype(jnp.float32)
    for device in others:
        image_sum += from_txt[device[1]].astype(jnp.float32)
    image_grad_ref[...] = image_sum

    for part in range(parts):
        pair_arrived(z, part)
        text_grad_ref[pieces[part]] = pair_sum(z, part)
    for source, there in far_first[::-1]:
        for part in range(parts):
            def add(source=source, part=part):
                arrived(
                    lambda: from_line.at[source, pieces[part]], lambda: line_sems.at[source, part]
                )
                text_grad_ref[pieces[part]] += from_line[source, pieces[part]].astype(jnp.float32)

            guarded(there, add)

    for condition, copy in sent:
        guarded(condition, lambda: copy().wait_send())


def local(n_img, n_txt, images, texts, labels):
    rows, width = images.shape
    length = n_img // 2
    image_rows = labels.shape[0]
    vmem = pl.BlockSpec(memory_space=pltpu.VMEM)
    hbm = pl.BlockSpec(memory_space=pltpu.HBM)
    low = jnp.bfloat16
    dma = pltpu.SemaphoreType.DMA
    sends = parts * (6 + 10 * length) + 3 * n_txt
    loss, image_grad, text_grad = pl.pallas_call(
        functools.partial(kernel, n_img, n_txt),
        out_shape=(
            jax.ShapeDtypeStruct((1, image_rows), jnp.float32),
            jax.ShapeDtypeStruct((rows, width), jnp.float32),
            jax.ShapeDtypeStruct((rows, width), jnp.float32),
        ),
        in_specs=[hbm, hbm, hbm],
        out_specs=(vmem, vmem, vmem),
        scratch_shapes=[
            pltpu.VMEM((1, image_rows), jnp.int32),
            pltpu.VMEM((rows, width), jnp.float32),
            pltpu.VMEM((rows, width), jnp.float32),
            pltpu.VMEM((n_txt, rows, width), low),
            pltpu.VMEM((2, length, rows, width), low),
            pltpu.VMEM((n_txt, 8, image_rows), jnp.float32),
            pltpu.VMEM((2, length, rows, width), low),
            pltpu.VMEM((length, rows, width), low),
            pltpu.VMEM((length, rows, width), low),
            pltpu.VMEM((length, rows, width), low),
            pltpu.VMEM((n_txt, rows, width), low),
            pltpu.VMEM((n_txt, rows, width), low),
            dma((3,)),
            dma((sends,)),
            dma((2, length, parts)),
            dma((n_txt,)),
            dma((n_txt,)),
            dma((length, parts)),
            dma((length, parts)),
            dma((n_txt,)),
        ],
        compiler_params=pltpu.CompilerParams(
            collective_id=0, has_side_effects=True, vmem_limit_bytes=48 * 1024 * 1024
        ),
    )(labels.reshape(1, image_rows), images, texts)
    return loss.reshape(image_rows), image_grad, text_grad


def solution(mesh):
    in_specs = (P(("img", "txt"), None), P(("txt", "img"), None), P("img"))
    out_specs = (P("img"), P(("img", "txt"), None), P(("txt", "img"), None))
    body = functools.partial(local, mesh.shape["img"], mesh.shape["txt"])
    return jax.shard_map(body, mesh=mesh, in_specs=in_specs, out_specs=out_specs, check_vma=False)
```

```python
import functools

import jax
import jax.numpy as jnp
from jax import lax
from jax.experimental import pallas as pl
from jax.experimental.pallas import tpu as pltpu
from jax.sharding import PartitionSpec as P

logit_scale = 100.0
MESH = pl.DeviceIdType.MESH
parts = 2


def kernel(
    n_img, n_txt,
    labels_hbm, images_hbm, texts_hbm,
    loss_ref, image_grad_ref, text_grad_ref,
    labels_ref, images_in, texts_in, img_panel, txt_panel, stats, text_terms, from_line,
    image_terms, from_plane,
    load_sems, send_sems, txt_sems, img_sems, label_sems, stat_sems, line_sems, plane_sems,
):
    length = n_img // 2
    rows, width = images_in.shape
    img, txt = lax.axis_index("img"), lax.axis_index("txt")
    z, y = img // 2, img % 2
    c = txt % 2
    flip = 1 - y
    across = (z * 2 + flip, txt)
    beside = txt - c + (1 - c)
    partner = (img, beside)
    piece = width // parts
    pieces = [pl.ds(part * piece, piece) for part in range(parts)]
    groups = [lax.rem(txt + 2 * k, n_txt) for k in range(1, n_txt // 2)]
    ways = []
    for way in (1, -1):
        ways.append((way, jnp.logical_and(z + way >= 0, z + way < length)))

    barrier = pltpu.get_barrier_semaphore()

    def greet(device):
        pl.semaphore_signal(barrier, inc=1, device_id=device, device_id_type=MESH)

    for device in [across, partner] + [(img, group) for group in groups]:
        greet(device)
    greeted = 2 + len(groups)
    for way, inside in ways:
        greeted += jnp.where(inside, 1, 0)
        pl.when(inside)(lambda: greet(((z + way) * 2 + y, txt)))

    loads = [
        pltpu.make_async_copy(texts_hbm, texts_in, load_sems.at[0]),
        pltpu.make_async_copy(images_hbm, images_in, load_sems.at[1]),
        pltpu.make_async_copy(labels_hbm, labels_ref.at[y], load_sems.at[2]),
    ]
    for load in loads:
        load.start()
    loads[0].wait()
    txt_panel[z] = texts_in[...].astype(jnp.bfloat16)
    loads[1].wait()
    img_panel[y, txt] = images_in[...].astype(jnp.bfloat16)
    loads[2].wait()
    pl.semaphore_wait(barrier, greeted)

    sent = []

    def guarded(condition, act):
        if condition is None:
            act()
        else:
            pl.when(condition)(act)

    def push(src, dst, arrival, device, condition=None):
        number = len(sent)

        def copy():
            return pltpu.make_async_remote_copy(
                src_ref=src(), dst_ref=dst(), send_sem=send_sems.at[number], recv_sem=arrival(),
                device_id=device, device_id_type=MESH,
            )

        sent.append((condition, copy))
        guarded(condition, lambda: copy().start())

    def arrived(ref, arrival, condition=None):
        def act():
            pltpu.make_async_remote_copy(
                src_ref=ref(), dst_ref=ref(), send_sem=send_sems.at[0], recv_sem=arrival(),
                device_id=across, device_id_type=MESH,
            ).wait_recv()

        guarded(condition, act)

    def same(ref, arrival, device, condition=None):
        push(ref, ref, arrival, device, condition)

    def text_at(source, part):
        return (lambda: txt_panel.at[source, :, pieces[part]], lambda: txt_sems.at[source, part])

    def image_at(side, source, part):
        return (
            lambda: img_panel.at[side, source, :, pieces[part]],
            lambda: img_sems.at[side, source, part],
        )

    for part in range(parts):
        for way, inside in ways:
            same(*text_at(z, part), ((z + way) * 2 + y, txt), inside)
        same(*image_at(y, txt, part), across)
        for group in groups:
            same(*image_at(y, txt, part), (img, group))
    same(lambda: labels_ref.at[y], lambda: label_sems.at[y], across)
    for part in range(parts):
        same(*image_at(y, txt, part), partner)

    def pass_text(step):
        for part in range(parts):
            for way, inside in ways:
                source = z - way * step
                there = jnp.logical_and(source >= 0, source < length)
                arrived(*text_at(source, part), there)
                same(
                    *text_at(source, part), ((z + way) * 2 + y, txt),
                    jnp.logical_and(there, inside),
                )

    def pass_images():
        for part in range(parts):
            arrived(*image_at(flip, txt, part))
            if part < parts // 2:
                for group in groups:
                    same(*image_at(flip, txt, part), (img, group))
            for group in groups:
                arrived(*image_at(y, group, part))
                if part >= parts // 2:
                    same(*image_at(y, group, part), across)
            same(*image_at(flip, txt, part), partner)
            for group in groups:
                same(*image_at(y, group, part), partner)

    for step in range(1, length):
        pass_text(step)
        if step == 1:
            pass_images()
        if step == 2 or length == 2:
            for group in groups:
                for part in range(parts):
                    arrived(*image_at(flip, group, part))
                    same(*image_at(flip, group, part), partner)
    others = [lax.rem(beside + 2 * k, n_txt) for k in range(n_txt // 2)]
    for source in others:
        for part in range(parts):
            for side in range(2):
                arrived(*image_at(side, source, part))
    arrived(lambda: labels_ref.at[flip], lambda: label_sems.at[flip])

    text_rows, image_rows = length * rows, n_txt * rows
    image_low = img_panel[...].reshape(2 * image_rows, width)
    text_low = txt_panel[...].reshape(text_rows, width)
    logits = logit_scale * lax.dot_general(
        text_low, image_low, (((1,), (1,)), ((), ())), preferred_element_type=jnp.float32
    )
    place = lax.broadcasted_iota(jnp.int32, (text_rows, 1), 0)
    column = txt * (n_img * rows) + ((place // rows) * 2 + y) * rows + place % rows
    hits = column == jnp.concatenate([labels_ref[0], labels_ref[1]], axis=1)
    highest = jnp.max(logits, axis=0, keepdims=True)
    exp_total = jnp.sum(jnp.exp(logits - highest), axis=0, keepdims=True)
    positive = jnp.sum(jnp.where(hits, logits, 0.0), axis=0, keepdims=True)
    line = lax.broadcasted_iota(jnp.int32, stats.shape[2:], 0)
    stats[y, txt] = jnp.where(
        line == 0, highest, jnp.where(line == 1, exp_total, jnp.where(line == 2, positive, 0.0))
    )
    plane = [(flip, group) for group in groups] + [(flip, source) for source in others]
    plane += [(flip, txt)] + [(y, group) for group in groups] + [(y, source) for source in others]
    for side, source in plane:
        same(
            lambda: stats.at[y, txt], lambda: stat_sems.at[y, txt], (z * 2 + side, source)
        )
    for side, source in plane:
        arrived(lambda: stats.at[side, source], lambda: stat_sems.at[side, source])
    every = stats[...].reshape(2 * n_txt, 8, 2 * image_rows)
    tops = every[:, 0:1, :]
    top = jnp.max(tops, axis=0)
    total = jnp.sum(every[:, 1:2, :] * jnp.exp(tops - top[None]), axis=0)
    log_total = top + jnp.log(total)
    grad_tile = (
        logit_scale * (jnp.exp(logits - log_total) - hits.astype(jnp.float32))
    ).astype(jnp.bfloat16)

    far_first = []
    for step in range(length - 1, 0, -1):
        for target in (z + step, z - step):
            far_first.append((target, jnp.logical_and(target >= 0, target < length)))
    text_terms[...] = (
        jnp.dot(grad_tile, image_low, preferred_element_type=jnp.float32)
        .astype(jnp.bfloat16)
        .reshape(length, rows, width)
    )
    for target, there in far_first:
        push(
            lambda target=target: text_terms.at[target], lambda: from_line.at[z],
            lambda: line_sems.at[z], (target * 2 + y, txt), there,
        )
    image_terms[...] = (
        lax.dot_general(
            grad_tile, text_low, (((0,), (0,)), ((), ())), preferred_element_type=jnp.float32
        )
        .astype(jnp.bfloat16)
        .reshape(2, n_txt, rows, width)
    )
    for side, target in plane:
        push(
            lambda side=side, target=target: image_terms.at[side, target],
            lambda: from_plane.at[y, txt], lambda: plane_sems.at[y, txt], (z * 2 + side, target),
        )

    losses = log_total - jnp.sum(every[:, 2:3, :], axis=0)
    loss_ref[...] = jnp.where(y == 0, losses[:, :image_rows], losses[:, image_rows:])
    text_grad_ref[...] = text_terms[z].astype(jnp.float32)
    image_grad_ref[...] = image_terms[y, txt].astype(jnp.float32)

    def add_text(source):
        arrived(lambda: from_line.at[source], lambda: line_sems.at[source])
        text_grad_ref[...] += from_line[source].astype(jnp.float32)

    def add_image(side, source):
        arrived(lambda: from_plane.at[side, source], lambda: plane_sems.at[side, source])
        image_grad_ref[...] += from_plane[side, source].astype(jnp.float32)

    for side, source in plane[::-1]:
        add_image(side, source)
    for source, there in far_first[::-1]:
        pl.when(there)(lambda: add_text(source))

    for condition, copy in sent:
        guarded(condition, lambda: copy().wait_send())


def local(n_img, n_txt, images, texts, labels):
    rows, width = images.shape
    length = n_img // 2
    image_rows = labels.shape[0]
    vmem = pl.BlockSpec(memory_space=pltpu.VMEM)
    hbm = pl.BlockSpec(memory_space=pltpu.HBM)
    low = jnp.bfloat16
    dma = pltpu.SemaphoreType.DMA
    sends = parts * (3 * length + 4 * n_txt) + 5 * n_txt + 2 * length
    loss, image_grad, text_grad = pl.pallas_call(
        functools.partial(kernel, n_img, n_txt),
        out_shape=(
            jax.ShapeDtypeStruct((1, image_rows), jnp.float32),
            jax.ShapeDtypeStruct((rows, width), jnp.float32),
            jax.ShapeDtypeStruct((rows, width), jnp.float32),
        ),
        in_specs=[hbm, hbm, hbm],
        out_specs=(vmem, vmem, vmem),
        scratch_shapes=[
            pltpu.VMEM((2, 1, image_rows), jnp.int32),
            pltpu.VMEM((rows, width), jnp.float32),
            pltpu.VMEM((rows, width), jnp.float32),
            pltpu.VMEM((2, n_txt, rows, width), low),
            pltpu.VMEM((length, rows, width), low),
            pltpu.VMEM((2, n_txt, 8, 2 * image_rows), jnp.float32),
            pltpu.VMEM((length, rows, width), low),
            pltpu.VMEM((length, rows, width), low),
            pltpu.VMEM((2, n_txt, rows, width), low),
            pltpu.VMEM((2, n_txt, rows, width), low),
            dma((3,)),
            dma((sends,)),
            dma((length, parts)),
            dma((2, n_txt, parts)),
            dma((2,)),
            dma((2, n_txt)),
            dma((length,)),
            dma((2, n_txt)),
        ],
        compiler_params=pltpu.CompilerParams(
            collective_id=0, has_side_effects=True, vmem_limit_bytes=48 * 1024 * 1024
        ),
    )(labels.reshape(1, image_rows), images, texts)
    return loss.reshape(image_rows), image_grad, text_grad


def solution(mesh):
    in_specs = (P(("img", "txt"), None), P(("txt", "img"), None), P("img"))
    out_specs = (P("img"), P(("img", "txt"), None), P(("txt", "img"), None))
    body = functools.partial(local, mesh.shape["img"], mesh.shape["txt"])
    return jax.shard_map(body, mesh=mesh, in_specs=in_specs, out_specs=out_specs, check_vma=False)
```

```python
import functools

import jax
import jax.numpy as jnp
from jax import lax
from jax.experimental import pallas as pl
from jax.experimental.pallas import tpu as pltpu
from jax.sharding import PartitionSpec as P

logit_scale = 100.0
MESH = pl.DeviceIdType.MESH
farthest = 3
parts = 2


def kernel(
    n_img, n_txt,
    labels_hbm, images_hbm, texts_hbm,
    loss_ref, image_grad_ref, text_grad_ref,
    labels_ref, images_in, texts_in, img_panel, txt_panel, stats, text_terms, from_line,
    image_terms, from_plane,
    load_sems, send_sems, near_sems, txt_sems, img_sems, label_sems, stat_sems, line_sems, plane_sems,
):
    length = n_img // 2
    rows, width = images_in.shape
    img, txt = lax.axis_index("img"), lax.axis_index("txt")
    z, y = img // 2, img % 2
    c = txt % 2
    flip = 1 - y
    across = (z * 2 + flip, txt)
    beside = txt - c + (1 - c)
    partner = (img, beside)
    piece = width // parts
    pieces = [pl.ds(part * piece, piece) for part in range(parts)]
    groups = [lax.rem(txt + 2 * k, n_txt) for k in range(1, n_txt // 2)]
    ways = []
    for way in (1, -1):
        ways.append((way, jnp.logical_and(z + way >= 0, z + way < length)))

    barrier = pltpu.get_barrier_semaphore()

    def greet(device):
        pl.semaphore_signal(barrier, inc=1, device_id=device, device_id_type=MESH)

    for device in [across, partner] + [(img, group) for group in groups]:
        greet(device)
    greeted = 2 + len(groups)
    for way, inside in ways:
        greeted += jnp.where(inside, 1, 0)
        pl.when(inside)(lambda: greet(((z + way) * 2 + y, txt)))

    loads = [
        pltpu.make_async_copy(texts_hbm, texts_in, load_sems.at[0]),
        pltpu.make_async_copy(images_hbm, images_in, load_sems.at[1]),
        pltpu.make_async_copy(labels_hbm, labels_ref.at[y], load_sems.at[2]),
    ]
    for load in loads:
        load.start()
    loads[0].wait()
    txt_panel[z] = texts_in[...].astype(jnp.bfloat16)
    loads[1].wait()
    img_panel[y, txt] = images_in[...].astype(jnp.bfloat16)
    loads[2].wait()
    pl.semaphore_wait(barrier, greeted)

    sent = []

    def guarded(condition, act):
        if condition is None:
            act()
        else:
            pl.when(condition)(act)

    def push(src, dst, arrival, device, condition=None):
        number = len(sent)

        def copy():
            return pltpu.make_async_remote_copy(
                src_ref=src(), dst_ref=dst(), send_sem=send_sems.at[number], recv_sem=arrival(),
                device_id=device, device_id_type=MESH,
            )

        sent.append((condition, copy))
        guarded(condition, lambda: copy().start())

    def arrived(ref, arrival, condition=None):
        def act():
            pltpu.make_async_remote_copy(
                src_ref=ref(), dst_ref=ref(), send_sem=send_sems.at[0], recv_sem=arrival(),
                device_id=across, device_id_type=MESH,
            ).wait_recv()

        guarded(condition, act)

    def same(ref, arrival, device, condition=None):
        push(ref, ref, arrival, device, condition)

    def text_at(source, part):
        return (lambda: txt_panel.at[source, :, pieces[part]], lambda: txt_sems.at[source, part])

    def image_at(side, source, part):
        return (
            lambda: img_panel.at[side, source, :, pieces[part]],
            lambda: img_sems.at[side, source, part],
        )

    def place_in(offset):
        return jnp.logical_and(z + offset >= 0, z + offset < length)

    def tell(reach):
        for way in (1, -1):
            @pl.when(jnp.logical_and(place_in(way * (reach - 1)), place_in(-way)))
            def _():
                pl.semaphore_signal(
                    near_sems.at[(1 - way) // 2, reach - 1], inc=1,
                    device_id=((z - way) * 2 + y, txt), device_id_type=MESH,
                )

    def told(reach):
        for way in (1, -1):
            @pl.when(place_in(way * reach))
            def _():
                pl.semaphore_wait(near_sems.at[(1 - way) // 2, reach - 1], 1)

    def text_to(source, part, offset, there=None):
        inside = place_in(offset)
        if there is not None:
            inside = jnp.logical_and(inside, there)
        same(*text_at(source, part), ((z + offset) * 2 + y, txt), inside)

    tell(2)
    for part in range(parts):
        for way in (1, -1):
            text_to(z, part, way)
        same(*image_at(y, txt, part), across)
        for group in groups:
            same(*image_at(y, txt, part), (img, group))
    same(lambda: labels_ref.at[y], lambda: label_sems.at[y], across)
    for part in range(parts):
        same(*image_at(y, txt, part), partner)

    for reach in range(2, farthest + 1):
        told(reach)
        if reach < farthest:
            tell(reach + 1)
        for part in range(parts):
            for way in (1, -1):
                text_to(z, part, way * reach)

    def pass_text(step):
        for part in range(parts):
            for way in (1, -1):
                source = z - way * step
                there = place_in(-way * step)
                arrived(*text_at(source, part), there)
                if step % farthest == 0:
                    for reach in range(1, farthest + 1):
                        if step + reach < length:
                            text_to(source, part, way * reach, there)

    def pass_images():
        for part in range(parts):
            arrived(*image_at(flip, txt, part))
            if part < parts // 2:
                for group in groups:
                    same(*image_at(flip, txt, part), (img, group))
            for group in groups:
                arrived(*image_at(y, group, part))
                if part >= parts // 2:
                    same(*image_at(y, group, part), across)
            same(*image_at(flip, txt, part), partner)
            for group in groups:
                same(*image_at(y, group, part), partner)

    for step in range(1, length):
        pass_text(step)
        if step == 1:
            pass_images()
        if step == 2 or length == 2:
            for group in groups:
                for part in range(parts):
                    arrived(*image_at(flip, group, part))
                    same(*image_at(flip, group, part), partner)
    others = [lax.rem(beside + 2 * k, n_txt) for k in range(n_txt // 2)]
    for source in others:
        for part in range(parts):
            for side in range(2):
                arrived(*image_at(side, source, part))
    arrived(lambda: labels_ref.at[flip], lambda: label_sems.at[flip])

    text_rows, image_rows = length * rows, n_txt * rows
    image_low = img_panel[...].reshape(2 * image_rows, width)
    text_low = txt_panel[...].reshape(text_rows, width)
    logits = logit_scale * lax.dot_general(
        text_low, image_low, (((1,), (1,)), ((), ())), preferred_element_type=jnp.float32
    )
    place = lax.broadcasted_iota(jnp.int32, (text_rows, 1), 0)
    column = txt * (n_img * rows) + ((place // rows) * 2 + y) * rows + place % rows
    hits = column == jnp.concatenate([labels_ref[0], labels_ref[1]], axis=1)
    highest = jnp.max(logits, axis=0, keepdims=True)
    exp_total = jnp.sum(jnp.exp(logits - highest), axis=0, keepdims=True)
    positive = jnp.sum(jnp.where(hits, logits, 0.0), axis=0, keepdims=True)
    line = lax.broadcasted_iota(jnp.int32, stats.shape[2:], 0)
    stats[y, txt] = jnp.where(
        line == 0, highest, jnp.where(line == 1, exp_total, jnp.where(line == 2, positive, 0.0))
    )
    plane = [(flip, group) for group in groups] + [(flip, source) for source in others]
    plane += [(flip, txt)] + [(y, group) for group in groups] + [(y, source) for source in others]
    for side, source in plane:
        same(
            lambda: stats.at[y, txt], lambda: stat_sems.at[y, txt], (z * 2 + side, source)
        )
    for side, source in plane:
        arrived(lambda: stats.at[side, source], lambda: stat_sems.at[side, source])
    every = stats[...].reshape(2 * n_txt, 8, 2 * image_rows)
    tops = every[:, 0:1, :]
    top = jnp.max(tops, axis=0)
    total = jnp.sum(every[:, 1:2, :] * jnp.exp(tops - top[None]), axis=0)
    log_total = top + jnp.log(total)
    grad_tile = (
        logit_scale * (jnp.exp(logits - log_total) - hits.astype(jnp.float32))
    ).astype(jnp.bfloat16)

    far_first = []
    for step in range(length - 1, 0, -1):
        for target in (z + step, z - step):
            far_first.append((target, jnp.logical_and(target >= 0, target < length)))
    text_terms[...] = (
        jnp.dot(grad_tile, image_low, preferred_element_type=jnp.float32)
        .astype(jnp.bfloat16)
        .reshape(length, rows, width)
    )
    for target, there in far_first:
        push(
            lambda target=target: text_terms.at[target], lambda: from_line.at[z],
            lambda: line_sems.at[z], (target * 2 + y, txt), there,
        )
    image_terms[...] = (
        lax.dot_general(
            grad_tile, text_low, (((0,), (0,)), ((), ())), preferred_element_type=jnp.float32
        )
        .astype(jnp.bfloat16)
        .reshape(2, n_txt, rows, width)
    )
    for side, target in plane:
        push(
            lambda side=side, target=target: image_terms.at[side, target],
            lambda: from_plane.at[y, txt], lambda: plane_sems.at[y, txt], (z * 2 + side, target),
        )

    losses = log_total - jnp.sum(every[:, 2:3, :], axis=0)
    loss_ref[...] = jnp.where(y == 0, losses[:, :image_rows], losses[:, image_rows:])
    text_grad_ref[...] = text_terms[z].astype(jnp.float32)
    image_grad_ref[...] = image_terms[y, txt].astype(jnp.float32)

    def add_text(source):
        arrived(lambda: from_line.at[source], lambda: line_sems.at[source])
        text_grad_ref[...] += from_line[source].astype(jnp.float32)

    def add_image(side, source):
        arrived(lambda: from_plane.at[side, source], lambda: plane_sems.at[side, source])
        image_grad_ref[...] += from_plane[side, source].astype(jnp.float32)

    for side, source in plane[::-1]:
        add_image(side, source)
    for source, there in far_first[::-1]:
        pl.when(there)(lambda: add_text(source))

    for condition, copy in sent:
        guarded(condition, lambda: copy().wait_send())


def local(n_img, n_txt, images, texts, labels):
    rows, width = images.shape
    length = n_img // 2
    image_rows = labels.shape[0]
    vmem = pl.BlockSpec(memory_space=pltpu.VMEM)
    hbm = pl.BlockSpec(memory_space=pltpu.HBM)
    low = jnp.bfloat16
    dma = pltpu.SemaphoreType.DMA
    sends = parts * (4 * length + 4 * n_txt + 2 * farthest) + 5 * n_txt + 2 * length
    loss, image_grad, text_grad = pl.pallas_call(
        functools.partial(kernel, n_img, n_txt),
        out_shape=(
            jax.ShapeDtypeStruct((1, image_rows), jnp.float32),
            jax.ShapeDtypeStruct((rows, width), jnp.float32),
            jax.ShapeDtypeStruct((rows, width), jnp.float32),
        ),
        in_specs=[hbm, hbm, hbm],
        out_specs=(vmem, vmem, vmem),
        scratch_shapes=[
            pltpu.VMEM((2, 1, image_rows), jnp.int32),
            pltpu.VMEM((rows, width), jnp.float32),
            pltpu.VMEM((rows, width), jnp.float32),
            pltpu.VMEM((2, n_txt, rows, width), low),
            pltpu.VMEM((length, rows, width), low),
            pltpu.VMEM((2, n_txt, 8, 2 * image_rows), jnp.float32),
            pltpu.VMEM((length, rows, width), low),
            pltpu.VMEM((length, rows, width), low),
            pltpu.VMEM((2, n_txt, rows, width), low),
            pltpu.VMEM((2, n_txt, rows, width), low),
            dma((3,)),
            dma((sends,)),
            pltpu.SemaphoreType.REGULAR((2, farthest)),
            dma((length, parts)),
            dma((2, n_txt, parts)),
            dma((2,)),
            dma((2, n_txt)),
            dma((length,)),
            dma((2, n_txt)),
        ],
        compiler_params=pltpu.CompilerParams(
            collective_id=0, has_side_effects=True, vmem_limit_bytes=48 * 1024 * 1024
        ),
    )(*[pltpu.with_memory_space_constraint(a, pltpu.HBM) for a in (labels.reshape(1, image_rows), images, texts)])
    return loss.reshape(image_rows), image_grad, text_grad


def solution(mesh):
    in_specs = (P(("img", "txt"), None), P(("txt", "img"), None), P("img"))
    out_specs = (P("img"), P(("img", "txt"), None), P(("txt", "img"), None))
    body = functools.partial(local, mesh.shape["img"], mesh.shape["txt"])
    return jax.shard_map(body, mesh=mesh, in_specs=in_specs, out_specs=out_specs, check_vma=False)
```

```python
import functools

import jax
import jax.numpy as jnp
from jax import lax
from jax.experimental import pallas as pl
from jax.experimental.pallas import tpu as pltpu
from jax.sharding import PartitionSpec as P

logit_scale = 100.0
MESH = pl.DeviceIdType.MESH
farthest = 3
parts = 1


def kernel(
    n_img, n_txt,
    labels_hbm, images_hbm, texts_hbm,
    loss_ref, image_grad_ref, text_grad_ref,
    labels_ref, images_in, texts_in, img_panel, txt_panel, stats, text_terms, from_line,
    image_terms, from_plane,
    load_sems, send_sems, near_sems, txt_sems, img_sems, label_sems, stat_sems, line_sems, plane_sems,
):
    length = n_img // 2
    rows, width = images_in.shape
    img, txt = lax.axis_index("img"), lax.axis_index("txt")
    z, y = img // 2, img % 2
    c = txt % 2
    flip = 1 - y
    across = (z * 2 + flip, txt)
    beside = txt - c + (1 - c)
    partner = (img, beside)
    piece = width // parts
    pieces = [pl.ds(part * piece, piece) for part in range(parts)]
    groups = [lax.rem(txt + 2 * k, n_txt) for k in range(1, n_txt // 2)]
    ways = []
    for way in (1, -1):
        ways.append((way, jnp.logical_and(z + way >= 0, z + way < length)))

    barrier = pltpu.get_barrier_semaphore()

    def greet(device):
        pl.semaphore_signal(barrier, inc=1, device_id=device, device_id_type=MESH)

    for device in [across, partner] + [(img, group) for group in groups]:
        greet(device)
    greeted = 2 + len(groups)
    for way, inside in ways:
        greeted += jnp.where(inside, 1, 0)
        pl.when(inside)(lambda: greet(((z + way) * 2 + y, txt)))

    loads = [
        pltpu.make_async_copy(texts_hbm, texts_in, load_sems.at[0]),
        pltpu.make_async_copy(images_hbm, images_in, load_sems.at[1]),
        pltpu.make_async_copy(labels_hbm, labels_ref.at[y], load_sems.at[2]),
    ]
    for load in loads:
        load.start()
    loads[0].wait()
    txt_panel[z] = texts_in[...].astype(jnp.bfloat16)
    loads[1].wait()
    img_panel[y, txt] = images_in[...].astype(jnp.bfloat16)
    loads[2].wait()
    pl.semaphore_wait(barrier, greeted)

    sent = []

    def guarded(condition, act):
        if condition is None:
            act()
        else:
            pl.when(condition)(act)

    def push(src, dst, arrival, device, condition=None):
        number = len(sent)

        def copy():
            return pltpu.make_async_remote_copy(
                src_ref=src(), dst_ref=dst(), send_sem=send_sems.at[number], recv_sem=arrival(),
                device_id=device, device_id_type=MESH,
            )

        sent.append((condition, copy))
        guarded(condition, lambda: copy().start())

    def arrived(ref, arrival, condition=None):
        def act():
            pltpu.make_async_remote_copy(
                src_ref=ref(), dst_ref=ref(), send_sem=send_sems.at[0], recv_sem=arrival(),
                device_id=across, device_id_type=MESH,
            ).wait_recv()

        guarded(condition, act)

    def same(ref, arrival, device, condition=None):
        push(ref, ref, arrival, device, condition)

    def text_at(source, part):
        return (lambda: txt_panel.at[source, :, pieces[part]], lambda: txt_sems.at[source, part])

    def image_at(side, source, part):
        return (
            lambda: img_panel.at[side, source, :, pieces[part]],
            lambda: img_sems.at[side, source, part],
        )

    def place_in(offset):
        return jnp.logical_and(z + offset >= 0, z + offset < length)

    def tell(reach):
        for way in (1, -1):
            @pl.when(jnp.logical_and(place_in(way * (reach - 1)), place_in(-way)))
            def _():
                pl.semaphore_signal(
                    near_sems.at[(1 - way) // 2, reach - 1], inc=1,
                    device_id=((z - way) * 2 + y, txt), device_id_type=MESH,
                )

    def told(reach):
        for way in (1, -1):
            @pl.when(place_in(way * reach))
            def _():
                pl.semaphore_wait(near_sems.at[(1 - way) // 2, reach - 1], 1)

    def text_to(source, part, offset, there=None):
        inside = place_in(offset)
        if there is not None:
            inside = jnp.logical_and(inside, there)
        same(*text_at(source, part), ((z + offset) * 2 + y, txt), inside)

    tell(2)
    for part in range(parts):
        for way in (1, -1):
            text_to(z, part, way)
        same(*image_at(y, txt, part), across)
        for group in groups:
            same(*image_at(y, txt, part), (img, group))
    same(lambda: labels_ref.at[y], lambda: label_sems.at[y], across)
    for part in range(parts):
        same(*image_at(y, txt, part), partner)

    for reach in range(2, farthest + 1):
        told(reach)
        if reach < farthest:
            tell(reach + 1)
        for part in range(parts):
            for way in (1, -1):
                text_to(z, part, way * reach)

    def pass_text(step):
        for part in range(parts):
            for way in (1, -1):
                source = z - way * step
                there = place_in(-way * step)
                arrived(*text_at(source, part), there)
                if step % farthest == 0:
                    for reach in range(1, farthest + 1):
                        if step + reach < length:
                            text_to(source, part, way * reach, there)

    def pass_images():
        for part in range(parts):
            arrived(*image_at(flip, txt, part))
            if part < parts // 2:
                for group in groups:
                    same(*image_at(flip, txt, part), (img, group))
            for group in groups:
                arrived(*image_at(y, group, part))
                if part >= parts // 2:
                    same(*image_at(y, group, part), across)
            same(*image_at(flip, txt, part), partner)
            for group in groups:
                same(*image_at(y, group, part), partner)

    for step in range(1, length):
        pass_text(step)
        if step == 1:
            pass_images()
        if step == 2 or length == 2:
            for group in groups:
                for part in range(parts):
                    arrived(*image_at(flip, group, part))
                    same(*image_at(flip, group, part), partner)
    others = [lax.rem(beside + 2 * k, n_txt) for k in range(n_txt // 2)]
    for source in others:
        for part in range(parts):
            for side in range(2):
                arrived(*image_at(side, source, part))
    arrived(lambda: labels_ref.at[flip], lambda: label_sems.at[flip])

    text_rows, image_rows = length * rows, n_txt * rows
    image_low = img_panel[...].reshape(2 * image_rows, width)
    text_low = txt_panel[...].reshape(text_rows, width)
    logits = logit_scale * lax.dot_general(
        text_low, image_low, (((1,), (1,)), ((), ())), preferred_element_type=jnp.float32
    )
    place = lax.broadcasted_iota(jnp.int32, (text_rows, 1), 0)
    column = txt * (n_img * rows) + ((place // rows) * 2 + y) * rows + place % rows
    hits = column == jnp.concatenate([labels_ref[0], labels_ref[1]], axis=1)
    highest = jnp.max(logits, axis=0, keepdims=True)
    exp_total = jnp.sum(jnp.exp(logits - highest), axis=0, keepdims=True)
    positive = jnp.sum(jnp.where(hits, logits, 0.0), axis=0, keepdims=True)
    line = lax.broadcasted_iota(jnp.int32, stats.shape[2:], 0)
    stats[y, txt] = jnp.where(
        line == 0, highest, jnp.where(line == 1, exp_total, jnp.where(line == 2, positive, 0.0))
    )
    plane = [(flip, group) for group in groups] + [(flip, source) for source in others]
    plane += [(flip, txt)] + [(y, group) for group in groups] + [(y, source) for source in others]
    for side, source in plane:
        same(
            lambda: stats.at[y, txt], lambda: stat_sems.at[y, txt], (z * 2 + side, source)
        )
    for side, source in plane:
        arrived(lambda: stats.at[side, source], lambda: stat_sems.at[side, source])
    every = stats[...].reshape(2 * n_txt, 8, 2 * image_rows)
    tops = every[:, 0:1, :]
    top = jnp.max(tops, axis=0)
    total = jnp.sum(every[:, 1:2, :] * jnp.exp(tops - top[None]), axis=0)
    log_total = top + jnp.log(total)
    grad_tile = (
        logit_scale * (jnp.exp(logits - log_total) - hits.astype(jnp.float32))
    ).astype(jnp.bfloat16)

    far_first = []
    for step in range(length - 1, 0, -1):
        for target in (z + step, z - step):
            far_first.append((target, jnp.logical_and(target >= 0, target < length)))
    text_terms[...] = (
        jnp.dot(grad_tile, image_low, preferred_element_type=jnp.float32)
        .astype(jnp.bfloat16)
        .reshape(length, rows, width)
    )
    for target, there in far_first:
        push(
            lambda target=target: text_terms.at[target], lambda: from_line.at[z],
            lambda: line_sems.at[z], (target * 2 + y, txt), there,
        )
    image_terms[...] = (
        lax.dot_general(
            grad_tile, text_low, (((0,), (0,)), ((), ())), preferred_element_type=jnp.float32
        )
        .astype(jnp.bfloat16)
        .reshape(2, n_txt, rows, width)
    )
    for side, target in plane:
        push(
            lambda side=side, target=target: image_terms.at[side, target],
            lambda: from_plane.at[y, txt], lambda: plane_sems.at[y, txt], (z * 2 + side, target),
        )

    losses = log_total - jnp.sum(every[:, 2:3, :], axis=0)
    loss_ref[...] = jnp.where(y == 0, losses[:, :image_rows], losses[:, image_rows:])
    text_grad_ref[...] = text_terms[z].astype(jnp.float32)
    image_grad_ref[...] = image_terms[y, txt].astype(jnp.float32)

    def add_text(source):
        arrived(lambda: from_line.at[source], lambda: line_sems.at[source])
        text_grad_ref[...] += from_line[source].astype(jnp.float32)

    def add_image(side, source):
        arrived(lambda: from_plane.at[side, source], lambda: plane_sems.at[side, source])
        image_grad_ref[...] += from_plane[side, source].astype(jnp.float32)

    for side, source in plane[::-1]:
        add_image(side, source)
    for source, there in far_first[::-1]:
        pl.when(there)(lambda: add_text(source))

    for condition, copy in sent:
        guarded(condition, lambda: copy().wait_send())


def local(n_img, n_txt, images, texts, labels):
    rows, width = images.shape
    length = n_img // 2
    image_rows = labels.shape[0]
    vmem = pl.BlockSpec(memory_space=pltpu.VMEM)
    hbm = pl.BlockSpec(memory_space=pltpu.HBM)
    low = jnp.bfloat16
    dma = pltpu.SemaphoreType.DMA
    sends = parts * (4 * length + 4 * n_txt + 2 * farthest) + 5 * n_txt + 2 * length
    loss, image_grad, text_grad = pl.pallas_call(
        functools.partial(kernel, n_img, n_txt),
        out_shape=(
            jax.ShapeDtypeStruct((1, image_rows), jnp.float32),
            jax.ShapeDtypeStruct((rows, width), jnp.float32),
            jax.ShapeDtypeStruct((rows, width), jnp.float32),
        ),
        in_specs=[hbm, hbm, hbm],
        out_specs=(vmem, vmem, vmem),
        scratch_shapes=[
            pltpu.VMEM((2, 1, image_rows), jnp.int32),
            pltpu.VMEM((rows, width), jnp.float32),
            pltpu.VMEM((rows, width), jnp.float32),
            pltpu.VMEM((2, n_txt, rows, width), low),
            pltpu.VMEM((length, rows, width), low),
            pltpu.VMEM((2, n_txt, 8, 2 * image_rows), jnp.float32),
            pltpu.VMEM((length, rows, width), low),
            pltpu.VMEM((length, rows, width), low),
            pltpu.VMEM((2, n_txt, rows, width), low),
            pltpu.VMEM((2, n_txt, rows, width), low),
            dma((3,)),
            dma((sends,)),
            pltpu.SemaphoreType.REGULAR((2, farthest)),
            dma((length, parts)),
            dma((2, n_txt, parts)),
            dma((2,)),
            dma((2, n_txt)),
            dma((length,)),
            dma((2, n_txt)),
        ],
        compiler_params=pltpu.CompilerParams(
            collective_id=0, has_side_effects=True, vmem_limit_bytes=48 * 1024 * 1024
        ),
    )(*[pltpu.with_memory_space_constraint(a, pltpu.HBM) for a in (labels.reshape(1, image_rows), images, texts)])
    return loss.reshape(image_rows), image_grad, text_grad


def solution(mesh):
    in_specs = (P(("img", "txt"), None), P(("txt", "img"), None), P("img"))
    out_specs = (P("img"), P(("img", "txt"), None), P(("txt", "img"), None))
    body = functools.partial(local, mesh.shape["img"], mesh.shape["txt"])
    return jax.shard_map(body, mesh=mesh, in_specs=in_specs, out_specs=out_specs, check_vma=False)
```
